32 devices in a mesh: dp: 8 (over z, x), tensor: 4 (over y, core).
Axes of the slice: x: 2, y: 2, z: 4, core: 2. Of those that a mesh axis runs over, the one named last changes fastest.
Arguments:
- tokens: bfloat16 [4096, 768], P(('dp', 'tensor')), may hold values from -6 to 6
- attn_gain: bfloat16 [768], P('dp'), may hold values from 0.25 to 1.75
- w_qkv: bfloat16 [3, 768, 768], P(None, 'dp', 'tensor'), may hold values from -14.072913 to 14.072913
- w_out: bfloat16 [768, 768], P('tensor', 'dp'), may hold values from -3 to 3
- mlp_gain: bfloat16 [768], P('dp'), may hold values from 0.25 to 1.75
- w_in: bfloat16 [2, 768, 1152], P(None, 'dp', 'tensor'), may hold values from -0.21875 to 0.21875
- w_down: bfloat16 [1152, 768], P('tensor', 'dp'), may hold values from -0.1875 to 0.1875
- cotangent: bfloat16 [4096, 768], P(('dp', 'tensor')), may hold values from -6 to 6
Outputs:
- out: bfloat16 [4096, 768], P(('dp', 'tensor'))
- input_grad: float32 [4096, 768], P(('dp', 'tensor'))
- attn_gain_grad: float32 [768], P('dp')
- w_qkv_grad: float32 [3, 768, 768], P(None, 'dp', 'tensor')
- w_out_grad: float32 [768, 768], P('tensor', 'dp')
- mlp_gain_grad: float32 [768], P('dp')
- w_in_grad: float32 [2, 768, 1152], P(None, 'dp', 'tensor')
- w_down_grad: float32 [1152, 768], P('tensor', 'dp')
The draws below stay inside these ranges and needn't reach their ends.
All inputs are finite; a program needn't handle non-finite values.
Results may differ from the reference program's by a relative error of at most 0.013.
Values may be sent and summed in bfloat16 or wider, within the bound.
A program may use at most 64 MiB of HBM per device.

```python
import jax
import jax.numpy as jnp
from jax import lax

D = 768
H = 12
HD = 64
FF = 1152
L = 512
TOKENS = 4096


def draw_w_qkv(key, part):
    first_key = jax.random.fold_in(key, 0)
    normal_part = jnp.clip(jax.random.normal(first_key, (3, D, D), jnp.float32), -6.0, 6.0) * D ** (-0.5)
    return normal_part.astype(jnp.bfloat16)


def raised(entries, rng, source, target, shards_of, factor):
    owner, partner = [(jnp.arange(entries.shape[dim]) // (entries.shape[dim] // shards_of)).reshape([-1 if axis == dim else 1 for axis in range(entries.ndim)]) for dim in (source, target)]
    chosen = jax.random.permutation(rng, shards_of)[partner]
    strong = (owner == chosen) | (owner == (partner + shards_of // 2) % shards_of)
    return jnp.where(strong, factor * entries, entries)


def level_of(rng, shape, pieces, smallest, largest):
    gain = 1.0
    for dim, parts in pieces:
        draws = jax.random.uniform(jax.random.fold_in(jax.random.fold_in(rng, 6), dim), (parts,), jnp.float32, smallest / len(pieces), largest / len(pieces))
        gain = gain * jnp.repeat(jnp.exp(draws), shape[dim] // parts).reshape((-1,) + (1,) * (len(shape) - 1 - dim))
    return gain


def gaussian(own_key, extent, width, limit, shards=(), dtype=jnp.bfloat16):
    values = width * jax.random.normal(own_key, extent, jnp.float32)
    if shards:
        values = values * level_of(own_key, extent, shards, -0.22, 0.18)
    return jnp.clip(values, -limit, limit).astype(dtype)


def heavy_noise(key, dims, scale, reach, cuts, heavy, kind=jnp.bfloat16):
    drawn = scale * jax.random.normal(key, dims, jnp.float32)
    if cuts:
        drawn = drawn * level_of(key, dims, cuts, -0.22, 0.18)
    return jnp.clip(raised(drawn, jax.random.fold_in(key, 3), *heavy), -reach, reach).astype(kind)


def setup_inputs(seed: int = 0) -> dict:
    key_of = jax.random.split(jax.random.key(seed), 9)
    tokens = heavy_noise(key_of[0], (TOKENS, D), 1.0, 6.0, ((0, 32),), (0, 1, 32, 2.75))
    attn_gain = jnp.clip(1.0 + 0.15 * jax.random.normal(key_of[1], (D,), jnp.float32), 0.25, 1.75).astype(jnp.bfloat16)
    w_qkv = draw_w_qkv(jax.random.fold_in(key_of[8], 71), 0)
    w_out = gaussian(key_of[3], (D, D), (max(D // 192, 1)) ** -0.5, 3.0, ((0, 4), (1, 8)))
    mlp_gain = jnp.clip(1.0 + 0.15 * jax.random.normal(key_of[4], (D,), jnp.float32), 0.25, 1.75).astype(jnp.bfloat16)
    w_in = gaussian(key_of[5], (2, D, FF), D ** -0.5, 0.21875, ((1, 8), (2, 4)))
    w_down = gaussian(key_of[6], (FF, D), FF ** -0.5, 0.1875, ((0, 4), (1, 8)))
    cotangent = heavy_noise(key_of[7], (TOKENS, D), 1.0, 6.0, ((0, 32),), (0, 1, 32, 2.75))
    return {"tokens": tokens, "attn_gain": attn_gain, "w_qkv": w_qkv, "w_out": w_out, "mlp_gain": mlp_gain, "w_in": w_in, "w_down": w_down, "cotangent": cotangent}


NORM_EPS = 1e-05
ROPE_THETA = 160000.0
SQRT_HALF = 0.7071067811865476
GAUSS_NORM = 0.3989422804014327

def widen_float(array):
    return lax.optimization_barrier(array).astype(jnp.float32)

def rope_tables(row_count):
    position = (jnp.arange(row_count) % L).astype(jnp.float32)
    halves = jnp.arange(HD // 2).astype(jnp.float32)
    inverse = ROPE_THETA ** (-2.0 * halves / HD)
    angles = position[:, None] * inverse[None, :]
    angles = jnp.concatenate([angles, angles], axis=1)
    return (jnp.cos(angles)[:, None, :], jnp.sin(angles)[:, None, :])

def rotate(field_rows, cos_table, sin_table):
    first_half = field_rows[..., :HD // 2]
    second_half = field_rows[..., HD // 2:]
    turned = jnp.concatenate([-second_half, first_half], axis=-1)
    return field_rows * cos_table + turned * sin_table

def rotate_back(grad_field, cos_table, sin_table):
    scaled = grad_field * sin_table
    turned = jnp.concatenate([scaled[..., HD // 2:], -scaled[..., :HD // 2]], axis=-1)
    return grad_field * cos_table + turned

def normalize(values):
    centred = values - lax.optimization_barrier(jnp.mean(values, axis=-1, keepdims=True))
    inv_std = lax.rsqrt(lax.optimization_barrier(jnp.mean(centred * centred, axis=-1, keepdims=True)) + NORM_EPS)
    return (centred * inv_std, inv_std)

def normalize_back(grad_norm, normed, inv_std, gain_row):
    gain_part = lax.optimization_barrier(jnp.sum(grad_norm * normed, axis=0))
    scaled = grad_norm * gain_row
    centred = scaled - lax.optimization_barrier(jnp.mean(scaled, axis=-1, keepdims=True))
    grad_in = inv_std * (centred - normed * lax.optimization_barrier(jnp.mean(scaled * normed, axis=-1, keepdims=True)))
    return (grad_in, gain_part)

def gelu_pair(inputs):
    normal_cdf = 0.5 * (1.0 + lax.erf(inputs * SQRT_HALF))
    return (inputs * normal_cdf, normal_cdf + inputs * jnp.exp(-0.5 * inputs * inputs) * GAUSS_NORM)

def attend(queries, key_rows, value_rows):
    score_scale = HD ** (-0.5)
    scores = jnp.einsum('qhd,khd->hqk', widen_float(queries), widen_float(key_rows)) * score_scale
    row_max = lax.optimization_barrier(jnp.max(scores, axis=-1, keepdims=True))
    log_total = row_max + jnp.log(lax.optimization_barrier(jnp.sum(jnp.exp(scores - row_max), axis=-1, keepdims=True)))
    weights = jnp.exp(scores - log_total).astype(jnp.bfloat16)
    attn_mix = jnp.einsum('hqk,khd->qhd', widen_float(weights), widen_float(value_rows)).astype(jnp.bfloat16)
    return (attn_mix, log_total)

def attend_back(queries, key_rows, value_rows, attn_mix, grad_mix, log_total):
    score_scale = HD ** (-0.5)
    scores = jnp.einsum('qhd,khd->hqk', widen_float(queries), widen_float(key_rows)) * score_scale
    probabilities = jnp.exp(scores - log_total)
    grad_probs = jnp.einsum('qhd,khd->hqk', widen_float(grad_mix), widen_float(value_rows))
    row_delta = lax.optimization_barrier(jnp.sum(widen_float(grad_mix) * widen_float(attn_mix), axis=-1))
    grad_scores = (probabilities * (grad_probs - jnp.transpose(row_delta)[:, :, None])).astype(jnp.bfloat16)
    prob_rounded = probabilities.astype(jnp.bfloat16)
    grad_values = jnp.einsum('hqk,qhd->khd', widen_float(prob_rounded), widen_float(grad_mix))
    grad_queries = jnp.einsum('hqk,khd->qhd', widen_float(grad_scores), widen_float(key_rows)) * score_scale
    grad_keys = jnp.einsum('hqk,qhd->khd', widen_float(grad_scores), widen_float(queries)) * score_scale
    return (grad_queries, grad_keys, grad_values)

def one_sequence(params, tok_rows, cot_rows, cos_table, sin_table):
    attn_gain, w_qkv, w_out, mlp_gain, w_in, w_down = params
    head_shape = (L, H, HD)
    residual = tok_rows.astype(jnp.float32)
    normed_one, inv_one = normalize(residual)
    ln_one = (normed_one * attn_gain.astype(jnp.float32)).astype(jnp.bfloat16)
    projections = [jnp.dot(ln_one, w_qkv[which], preferred_element_type=jnp.float32) for which in range(3)]
    queries = rotate(projections[0].reshape(head_shape), cos_table, sin_table).astype(jnp.bfloat16)
    key_rows = rotate(projections[1].reshape(head_shape), cos_table, sin_table).astype(jnp.bfloat16)
    value_rows = projections[2].reshape(head_shape).astype(jnp.bfloat16)
    attn_mix, log_total = attend(queries, key_rows, value_rows)
    mixed_rows = attn_mix.reshape(L, D)
    hidden_res = residual + jnp.dot(mixed_rows, w_out, preferred_element_type=jnp.float32)
    normed_two, inv_two = normalize(hidden_res)
    ln_two = (normed_two * mlp_gain.astype(jnp.float32)).astype(jnp.bfloat16)
    input_part = jnp.dot(ln_two, w_in[0], preferred_element_type=jnp.float32)
    gate_part = jnp.dot(ln_two, w_in[1], preferred_element_type=jnp.float32)
    activated, gelu_slope = gelu_pair(input_part)
    hidden_act = (activated * gate_part).astype(jnp.bfloat16)
    output = (hidden_res + jnp.dot(hidden_act, w_down, preferred_element_type=jnp.float32)).astype(jnp.bfloat16)
    grad_down = jnp.dot(hidden_act.T, cot_rows, preferred_element_type=jnp.float32)
    grad_act = jnp.dot(cot_rows, w_down.T, preferred_element_type=jnp.float32)
    grad_input_part = (grad_act * gate_part * gelu_slope).astype(jnp.bfloat16)
    grad_gate_part = (grad_act * activated).astype(jnp.bfloat16)
    grad_in = jnp.stack([jnp.dot(ln_two.T, grad_input_part, preferred_element_type=jnp.float32), jnp.dot(ln_two.T, grad_gate_part, preferred_element_type=jnp.float32)])
    grad_ln_two = jnp.dot(grad_input_part, w_in[0].T, preferred_element_type=jnp.float32) + jnp.dot(grad_gate_part, w_in[1].T, preferred_element_type=jnp.float32)
    grad_res_two, mlp_gain_part = normalize_back(grad_ln_two, normed_two, inv_two, mlp_gain.astype(jnp.float32))
    grad_hidden = cot_rows.astype(jnp.float32) + grad_res_two
    grad_hidden_bf = grad_hidden.astype(jnp.bfloat16)
    grad_out = jnp.dot(mixed_rows.T, grad_hidden_bf, preferred_element_type=jnp.float32)
    grad_mix = jnp.dot(grad_hidden_bf, w_out.T, preferred_element_type=jnp.float32).astype(jnp.bfloat16).reshape(head_shape)
    grad_q, grad_k, grad_v = attend_back(queries, key_rows, value_rows, attn_mix, grad_mix, log_total)
    grad_proj = [rotate_back(grad_q, cos_table, sin_table).reshape(L, D).astype(jnp.bfloat16), rotate_back(grad_k, cos_table, sin_table).reshape(L, D).astype(jnp.bfloat16), grad_v.reshape(L, D).astype(jnp.bfloat16)]
    grad_qkv = jnp.stack([jnp.dot(ln_one.T, grad_proj[which], preferred_element_type=jnp.float32) for which in range(3)])
    grad_ln_one = jnp.dot(grad_proj[0], w_qkv[0].T, preferred_element_type=jnp.float32)
    grad_ln_one = grad_ln_one + jnp.dot(grad_proj[1], w_qkv[1].T, preferred_element_type=jnp.float32)
    grad_ln_one = grad_ln_one + jnp.dot(grad_proj[2], w_qkv[2].T, preferred_element_type=jnp.float32)
    grad_res_one, attn_gain_part = normalize_back(grad_ln_one, normed_one, inv_one, attn_gain.astype(jnp.float32))
    input_grad = grad_hidden + grad_res_one
    return (output, input_grad, (attn_gain_part, grad_qkv, grad_out, mlp_gain_part, grad_in, grad_down))

def reference(tokens, attn_gain, w_qkv, w_out, mlp_gain, w_in, w_down, cotangent):
    seq_count = tokens.shape[0] // L
    cos_table, sin_table = rope_tables(L)
    params = (attn_gain, w_qkv, w_out, mlp_gain, w_in, w_down)

    def one_step(totals, seq_pair):
        tok_rows, cot_rows = seq_pair
        output, input_grad, seq_grads = one_sequence(params, tok_rows, cot_rows, cos_table, sin_table)
        return (jax.tree.map(lambda left, right: left + right, totals, seq_grads), (output, input_grad))
    zero_grads = (jnp.zeros((D,), jnp.float32), jnp.zeros((3, D, D), jnp.float32), jnp.zeros((D, D), jnp.float32), jnp.zeros((D,), jnp.float32), jnp.zeros((2, D, FF), jnp.float32), jnp.zeros((FF, D), jnp.float32))
    totals, (outputs, input_grads) = lax.scan(one_step, zero_grads, (tokens.reshape(seq_count, L, D), cotangent.reshape(seq_count, L, D)))
    return (outputs.reshape(seq_count * L, D), input_grads.reshape(seq_count * L, D), totals[0], totals[1], totals[2], totals[3], totals[4], totals[5])
```

```python
import functools

import jax
import jax.numpy as jnp
from jax import lax
from jax.experimental import pallas as pl
from jax.experimental.pallas import tpu as pltpu
from jax.sharding import PartitionSpec as P

HD = 64
L = 512


NORM_EPS = 1e-05
ROPE_THETA = 160000.0
SQRT_HALF = 0.7071067811865476
GAUSS_NORM = 0.3989422804014327


def rope_tables(row_count):
    position = (jnp.arange(row_count) % L).astype(jnp.float32)
    halves = jnp.arange(HD // 2).astype(jnp.float32)
    inverse = ROPE_THETA ** (-2.0 * halves / HD)
    angles = position[:, None] * inverse[None, :]
    angles = jnp.concatenate([angles, angles], axis=1)
    return (jnp.cos(angles)[:, None, :], jnp.sin(angles)[:, None, :])


def rotate(field_rows, cos_table, sin_table):
    first_half = field_rows[..., : HD // 2]
    second_half = field_rows[..., HD // 2 :]
    turned = jnp.concatenate([-second_half, first_half], axis=-1)
    return field_rows * cos_table + turned * sin_table


def rotate_back(grad_field, cos_table, sin_table):
    scaled = grad_field * sin_table
    turned = jnp.concatenate([scaled[..., HD // 2 :], -scaled[..., : HD // 2]], axis=-1)
    return grad_field * cos_table + turned


def normalize(values):
    centred = values - jnp.mean(values, axis=-1, keepdims=True)
    inv_std = lax.rsqrt(jnp.mean(centred * centred, axis=-1, keepdims=True) + NORM_EPS)
    return (centred * inv_std, inv_std)


def normalize_back(grad_norm, normed, inv_std, gain_row):
    gain_part = jnp.sum(grad_norm * normed, axis=0)
    scaled = grad_norm * gain_row
    centred = scaled - jnp.mean(scaled, axis=-1, keepdims=True)
    grad_in = inv_std * (centred - normed * jnp.mean(scaled * normed, axis=-1, keepdims=True))
    return (grad_in, gain_part)


def gelu_pair(inputs):
    normal_cdf = 0.5 * (1.0 + lax.erf(inputs * SQRT_HALF))
    return (inputs * normal_cdf, normal_cdf + inputs * jnp.exp(-0.5 * inputs * inputs) * GAUSS_NORM)


def attend(queries, key_rows, value_rows):
    score_scale = HD ** (-0.5)
    scores = (
        jnp.einsum("qhd,khd->hqk", queries, key_rows, preferred_element_type=jnp.float32)
        * score_scale
    )
    row_max = jnp.max(scores, axis=-1, keepdims=True)
    log_total = row_max + jnp.log(jnp.sum(jnp.exp(scores - row_max), axis=-1, keepdims=True))
    weights = jnp.exp(scores - log_total).astype(jnp.bfloat16)
    attn_mix = jnp.einsum(
        "hqk,khd->qhd", weights, value_rows, preferred_element_type=jnp.float32
    ).astype(jnp.bfloat16)
    return (attn_mix, log_total)


def attend_back(queries, key_rows, value_rows, attn_mix, grad_mix, log_total):
    score_scale = HD ** (-0.5)
    scores = (
        jnp.einsum("qhd,khd->hqk", queries, key_rows, preferred_element_type=jnp.float32)
        * score_scale
    )
    probabilities = jnp.exp(scores - log_total)
    grad_probs = jnp.einsum(
        "qhd,khd->hqk", grad_mix, value_rows, preferred_element_type=jnp.float32
    )
    row_delta = jnp.sum(grad_mix.astype(jnp.float32) * attn_mix.astype(jnp.float32), axis=-1)
    grad_scores = (probabilities * (grad_probs - jnp.transpose(row_delta)[:, :, None])).astype(
        jnp.bfloat16
    )
    prob_rounded = probabilities.astype(jnp.bfloat16)
    grad_values = jnp.einsum(
        "hqk,qhd->khd", prob_rounded, grad_mix, preferred_element_type=jnp.float32
    )
    grad_queries = (
        jnp.einsum("hqk,khd->qhd", grad_scores, key_rows, preferred_element_type=jnp.float32)
        * score_scale
    )
    grad_keys = (
        jnp.einsum("hqk,qhd->khd", grad_scores, queries, preferred_element_type=jnp.float32)
        * score_scale
    )
    return (grad_queries, grad_keys, grad_values)


def exchange_kernel(plan, sizes, *refs):
    count = len(plan)
    sources, targets = refs[:count], refs[count : 2 * count]
    own_sem, send_sem, recv_sem = refs[2 * count :]
    axes = sorted({axis for _, axis in plan})
    barrier = pltpu.get_barrier_semaphore()
    total = 0
    for axis in axes:
        me = lax.axis_index(axis)
        for shift in range(1, sizes[axis]):
            pl.semaphore_signal(
                barrier,
                inc=1,
                device_id={axis: lax.rem(me + shift, sizes[axis])},
                device_id_type=pl.DeviceIdType.MESH,
            )
            total += 1
    pl.semaphore_wait(barrier, total)
    slot = 0
    pending, relays, local = [], [], []

    def remote(source, target, axis, peer, index):
        return pltpu.make_async_remote_copy(
            src_ref=source,
            dst_ref=target,
            send_sem=send_sem.at[index],
            recv_sem=recv_sem.at[index],
            device_id={axis: peer},
            device_id_type=pl.DeviceIdType.MESH,
        )

    for which, (kind, axis) in enumerate(plan):
        size = sizes[axis]
        me = lax.axis_index(axis)
        source, target = sources[which], targets[which]
        if kind == "relay":
            outer = size // 2
            column = lax.rem(me, 2)
            row = me // 2
            partner = row * 2 + 1 - column
            for shift in range(1, outer):
                peer = lax.rem(row + shift, outer) * 2 + column
                copy = remote(source, target.at[me], axis, peer, slot)
                copy.start()
                origin = lax.rem(row + outer - shift, outer) * 2 + column
                relays.append((copy, target, axis, origin, partner, slot + 1))
                slot += 2
            copy = remote(source, target.at[me], axis, partner, slot)
            copy.start()
            pending.append(copy)
            slot += 1
        else:
            for shift in range(1, size):
                peer = lax.rem(me + shift, size)
                piece = source if kind == "gather" else source.at[peer]
                copy = remote(piece, target.at[me], axis, peer, slot)
                copy.start()
                pending.append(copy)
                slot += 1
        piece = source if kind != "scatter" else source.at[me]
        copy = pltpu.make_async_copy(piece, target.at[me], own_sem.at[which])
        copy.start()
        local.append(copy)
    for copy, target, axis, origin, partner, index in relays:
        copy.wait_recv()
        onward = remote(target.at[origin], target.at[origin], axis, partner, index)
        onward.start()
        pending.append(onward)
    for copy, *_ in relays:
        copy.wait_send()
    for copy in pending + local:
        copy.wait()


def slots_of(kind, size):
    return 2 * (size // 2 - 1) + 1 if kind == "relay" else size - 1


def exchange(sizes, number, *ops):
    plan = tuple((kind, axis) for kind, axis, _ in ops)
    arrays = [array for _, _, array in ops]
    shapes = [
        jax.ShapeDtypeStruct(
            array.shape if kind == "scatter" else (sizes[axis],) + array.shape, array.dtype
        )
        for kind, axis, array in ops
    ]
    slots = sum(slots_of(kind, sizes[axis]) for kind, axis in plan)
    return pl.pallas_call(
        functools.partial(exchange_kernel, plan, sizes),
        out_shape=shapes,
        in_specs=[pl.BlockSpec(memory_space=pltpu.VMEM)] * len(arrays),
        out_specs=[pl.BlockSpec(memory_space=pltpu.VMEM)] * len(arrays),
        scratch_shapes=[
            pltpu.SemaphoreType.DMA((len(arrays),)),
            pltpu.SemaphoreType.DMA((slots,)),
            pltpu.SemaphoreType.DMA((slots,)),
        ],
        compiler_params=pltpu.CompilerParams(
            collective_id=number, has_side_effects=True, vmem_limit_bytes=48 << 20
        ),
    )(*arrays)


def pad_columns(array, multiple=128):
    extra = -array.shape[-1] % multiple
    return jnp.pad(array, [(0, 0)] * (array.ndim - 1) + [(0, extra)])


def total_of(pieces):
    return jnp.sum(pieces.astype(jnp.float32), axis=0)


def dot_f32(left, right, left_dim, right_dim):
    return lax.dot_general(
        left, right, (((left_dim,), (right_dim,)), ((), ())), preferred_element_type=jnp.float32
    )


def body(sizes, tokens, attn_gain, w_qkv, w_out, mlp_gain, w_in, w_down, cotangent):
    bf16, f32 = jnp.bfloat16, jnp.float32
    groups, members = sizes["dp"], sizes["tensor"]
    block = w_qkv.shape[1]
    width = block * groups
    heads_wide, hidden = w_qkv.shape[2], w_in.shape[2]
    own_rows = tokens.shape[0]
    packed = pad_columns(
        jnp.concatenate(
            [w_qkv[0], w_qkv[1], w_qkv[2], w_out.T, w_in[0], w_in[1], w_down.T]
            + [attn_gain[:, None], mlp_gain[:, None]],
            axis=1,
        )
    )
    weights, token_rows, grad_rows = exchange(
        sizes,
        0,
        ("relay", "dp", packed),
        ("gather", "tensor", tokens),
        ("gather", "tensor", cotangent),
    )
    weights = weights.reshape(width, -1)
    edges = [3 * heads_wide, 4 * heads_wide, 4 * heads_wide + 2 * hidden, 4 * heads_wide + 3 * hidden]
    qkv_weight = weights[:, : edges[0]]
    out_weight_t = weights[:, edges[0] : edges[1]]
    in_weight = weights[:, edges[1] : edges[2]]
    down_weight_t = weights[:, edges[2] : edges[3]]
    gains = weights[:, edges[3] : edges[3] + 2].astype(f32).T
    attn_full, mlp_full = gains[0:1], gains[1:2]
    row_count = own_rows * members
    grad_rows = grad_rows.reshape(row_count, width)
    residual = tokens.astype(f32)
    normed_one, inv_one = normalize(residual)
    rows_one = (normalize(token_rows.reshape(row_count, width).astype(f32))[0] * attn_full).astype(bf16)
    head_count = heads_wide // HD
    head_shape = (row_count, head_count, HD)
    seq_shape = (row_count // L, L, head_count, HD)
    flat_shape = (row_count, heads_wide)
    cos_table, sin_table = rope_tables(row_count)
    projected = dot_f32(rows_one, qkv_weight, 1, 0)
    pieces = [projected[:, i * heads_wide : (i + 1) * heads_wide].reshape(head_shape) for i in range(3)]
    queries = rotate(pieces[0], cos_table, sin_table).astype(bf16).reshape(seq_shape)
    key_rows = rotate(pieces[1], cos_table, sin_table).astype(bf16).reshape(seq_shape)
    value_rows = pieces[2].astype(bf16).reshape(seq_shape)
    one_seq = row_count == L

    def over_sequences(function, arrays):
        if one_seq:
            results = function(*[array[0] for array in arrays])
            return tuple(result[None] for result in results)
        return lax.map(lambda seq_block: function(*seq_block), arrays)

    attn_mix, log_total = over_sequences(attend, (queries, key_rows, value_rows))
    mixed_rows = attn_mix.reshape(flat_shape)
    attn_part = dot_f32(mixed_rows, out_weight_t, 1, 1).astype(bf16)
    (attn_parts,) = exchange(
        sizes, 1, ("scatter", "tensor", attn_part.reshape(members, own_rows, width))
    )
    hidden_res = residual + total_of(attn_parts)
    normed_two, inv_two = normalize(hidden_res)
    ln_two = (normed_two * mlp_full).astype(bf16)
    (rows_two,) = exchange(sizes, 2, ("gather", "tensor", ln_two))
    rows_two = rows_two.reshape(row_count, width)
    up_gate = dot_f32(rows_two, in_weight, 1, 0)
    activated, gelu_slope = gelu_pair(up_gate[:, :hidden])
    gate_part = up_gate[:, hidden:]
    hidden_act = (activated * gate_part).astype(bf16)
    mlp_part = dot_f32(hidden_act, down_weight_t, 1, 1).astype(bf16)
    grad_down_t = dot_f32(grad_rows, hidden_act, 0, 0).astype(bf16)
    grad_act = dot_f32(grad_rows, down_weight_t, 1, 0)
    grad_up_gate = jnp.concatenate(
        [(grad_act * gate_part * gelu_slope).astype(bf16), (grad_act * activated).astype(bf16)], axis=1
    )
    grad_in = dot_f32(rows_two, grad_up_gate, 0, 0).astype(bf16)
    ln_two_part = dot_f32(grad_up_gate, in_weight, 1, 1).astype(bf16)
    mlp_parts, ln_two_parts, grad_down_parts = exchange(
        sizes,
        3,
        ("scatter", "tensor", mlp_part.reshape(members, own_rows, width)),
        ("scatter", "tensor", ln_two_part.reshape(members, own_rows, width)),
        ("scatter", "dp", pad_columns(grad_down_t).reshape(groups, block, -1)),
    )
    output = (hidden_res + total_of(mlp_parts)).astype(bf16)
    grad_res_two, mlp_gain_part = normalize_back(total_of(ln_two_parts), normed_two, inv_two, mlp_full)
    grad_hidden = cotangent.astype(f32) + grad_res_two
    half = hidden
    grad_hidden_rows, grad_in_parts_a = exchange(
        sizes,
        4,
        ("gather", "tensor", grad_hidden.astype(bf16)),
        ("scatter", "dp", pad_columns(grad_in[:, :half]).reshape(groups, block, -1)),
    )
    grad_hidden_rows = grad_hidden_rows.reshape(row_count, width)
    grad_out_t = dot_f32(grad_hidden_rows, mixed_rows, 0, 0).astype(bf16)
    grad_mix = dot_f32(grad_hidden_rows, out_weight_t, 1, 0).astype(bf16).reshape(seq_shape)
    grad_q, grad_k, grad_v = over_sequences(
        attend_back, (queries, key_rows, value_rows, attn_mix, grad_mix, log_total)
    )
    grad_proj = jnp.concatenate(
        [
            rotate_back(grad_q.reshape(head_shape), cos_table, sin_table).reshape(flat_shape),
            rotate_back(grad_k.reshape(head_shape), cos_table, sin_table).reshape(flat_shape),
            grad_v.reshape(flat_shape),
        ],
        axis=1,
    ).astype(bf16)
    grad_qkv = dot_f32(rows_one, grad_proj, 0, 0).astype(bf16)
    ln_one_part = dot_f32(grad_proj, qkv_weight, 1, 1).astype(bf16)
    ln_one_parts, grad_in_parts_b = exchange(
        sizes,
        5,
        ("scatter", "tensor", ln_one_part.reshape(members, own_rows, width)),
        ("scatter", "dp", pad_columns(grad_in[:, half:]).reshape(groups, block, -1)),
    )
    grad_res_one, attn_gain_part = normalize_back(total_of(ln_one_parts), normed_one, inv_one, attn_full)
    input_grad = grad_hidden + grad_res_one
    gain_parts = jnp.stack([attn_gain_part, mlp_gain_part] + [jnp.zeros_like(attn_gain_part)] * 6)
    gain_parts = pad_columns(jnp.swapaxes(gain_parts.reshape(8, groups, block), 0, 1))
    late_parts, gain_parts = exchange(
        sizes,
        6,
        ("scatter", "dp", jnp.concatenate([grad_qkv, grad_out_t], axis=1).reshape(groups, block, -1)),
        ("scatter", "dp", gain_parts),
    )
    (gain_groups,) = exchange(sizes, 7, ("gather", "tensor", total_of(gain_parts)))
    gain_sum = total_of(gain_groups)
    late = total_of(late_parts)
    grad_w_qkv = jnp.stack([late[:, i * heads_wide : (i + 1) * heads_wide] for i in range(3)])
    grad_w_out = late[:, 3 * heads_wide : 4 * heads_wide].T
    grad_w_in = jnp.stack([total_of(grad_in_parts_a)[:, :hidden], total_of(grad_in_parts_b)[:, :hidden]])
    grad_w_down = total_of(grad_down_parts)[:, :hidden].T
    return (
        output,
        input_grad,
        gain_sum[0, :block],
        grad_w_qkv,
        grad_w_out,
        gain_sum[1, :block],
        grad_w_in,
        grad_w_down,
    )


def solution(mesh):
    in_specs = (
        P(("dp", "tensor"), None),
        P("dp"),
        P(None, "dp", "tensor"),
        P("tensor", "dp"),
        P("dp"),
        P(None, "dp", "tensor"),
        P("tensor", "dp"),
        P(("dp", "tensor"), None),
    )
    out_specs = (
        P(("dp", "tensor"), None),
        P(("dp", "tensor"), None),
        P("dp"),
        P(None, "dp", "tensor"),
        P("tensor", "dp"),
        P("dp"),
        P(None, "dp", "tensor"),
        P("tensor", "dp"),
    )
    sizes = {axis: mesh.shape[axis] for axis in ("dp", "tensor")}
    return jax.shard_map(functools.partial(body, sizes), mesh=mesh, in_specs=in_specs, out_specs=out_specs, check_vma=False)
```

```python
import functools

import jax
import jax.numpy as jnp
from jax import lax
from jax.experimental import pallas as pl
from jax.experimental.pallas import tpu as pltpu
from jax.sharding import PartitionSpec as P

HD = 64
L = 512


NORM_EPS = 1e-05
ROPE_THETA = 160000.0
SQRT_HALF = 0.7071067811865476
GAUSS_NORM = 0.3989422804014327


def rope_tables(row_count):
    position = (jnp.arange(row_count) % L).astype(jnp.float32)
    halves = jnp.arange(HD // 2).astype(jnp.float32)
    inverse = ROPE_THETA ** (-2.0 * halves / HD)
    angles = position[:, None] * inverse[None, :]
    angles = jnp.concatenate([angles, angles], axis=1)
    return (jnp.cos(angles)[:, None, :], jnp.sin(angles)[:, None, :])


def rotate(field_rows, cos_table, sin_table):
    first_half = field_rows[..., : HD // 2]
    second_half = field_rows[..., HD // 2 :]
    turned = jnp.concatenate([-second_half, first_half], axis=-1)
    return field_rows * cos_table + turned * sin_table


def rotate_back(grad_field, cos_table, sin_table):
    scaled = grad_field * sin_table
    turned = jnp.concatenate([scaled[..., HD // 2 :], -scaled[..., : HD // 2]], axis=-1)
    return grad_field * cos_table + turned


def normalize(values):
    centred = values - jnp.mean(values, axis=-1, keepdims=True)
    inv_std = lax.rsqrt(jnp.mean(centred * centred, axis=-1, keepdims=True) + NORM_EPS)
    return (centred * inv_std, inv_std)


def normalize_back(grad_norm, normed, inv_std, gain_row):
    gain_part = jnp.sum(grad_norm * normed, axis=0)
    scaled = grad_norm * gain_row
    centred = scaled - jnp.mean(scaled, axis=-1, keepdims=True)
    grad_in = inv_std * (centred - normed * jnp.mean(scaled * normed, axis=-1, keepdims=True))
    return (grad_in, gain_part)


def gelu_pair(inputs):
    normal_cdf = 0.5 * (1.0 + lax.erf(inputs * SQRT_HALF))
    return (inputs * normal_cdf, normal_cdf + inputs * jnp.exp(-0.5 * inputs * inputs) * GAUSS_NORM)


def attend(queries, key_rows, value_rows):
    score_scale = HD ** (-0.5)
    scores = (
        jnp.einsum("qhd,khd->hqk", queries, key_rows, preferred_element_type=jnp.float32)
        * score_scale
    )
    row_max = jnp.max(scores, axis=-1, keepdims=True)
    log_total = row_max + jnp.log(jnp.sum(jnp.exp(scores - row_max), axis=-1, keepdims=True))
    weights = jnp.exp(scores - log_total).astype(jnp.bfloat16)
    attn_mix = jnp.einsum(
        "hqk,khd->qhd", weights, value_rows, preferred_element_type=jnp.float32
    ).astype(jnp.bfloat16)
    return (attn_mix, log_total)


def attend_back(queries, key_rows, value_rows, attn_mix, grad_mix, log_total):
    score_scale = HD ** (-0.5)
    scores = (
        jnp.einsum("qhd,khd->hqk", queries, key_rows, preferred_element_type=jnp.float32)
        * score_scale
    )
    probabilities = jnp.exp(scores - log_total)
    grad_probs = jnp.einsum(
        "qhd,khd->hqk", grad_mix, value_rows, preferred_element_type=jnp.float32
    )
    row_delta = jnp.sum(grad_mix.astype(jnp.float32) * attn_mix.astype(jnp.float32), axis=-1)
    grad_scores = (probabilities * (grad_probs - jnp.transpose(row_delta)[:, :, None])).astype(
        jnp.bfloat16
    )
    prob_rounded = probabilities.astype(jnp.bfloat16)
    grad_values = jnp.einsum(
        "hqk,qhd->khd", prob_rounded, grad_mix, preferred_element_type=jnp.float32
    )
    grad_queries = (
        jnp.einsum("hqk,khd->qhd", grad_scores, key_rows, preferred_element_type=jnp.float32)
        * score_scale
    )
    grad_keys = (
        jnp.einsum("hqk,qhd->khd", grad_scores, queries, preferred_element_type=jnp.float32)
        * score_scale
    )
    return (grad_queries, grad_keys, grad_values)


def exchange_kernel(plan, sizes, *refs):
    count = len(plan)
    sources, targets = refs[:count], refs[count : 2 * count]
    own_sem, send_sem, recv_sem = refs[2 * count :]
    axes = sorted({axis for _, axis, _ in plan})
    barrier = pltpu.get_barrier_semaphore()
    total = 0
    for axis in axes:
        me = lax.axis_index(axis)
        for shift in range(1, sizes[axis]):
            pl.semaphore_signal(
                barrier,
                inc=1,
                device_id={axis: lax.rem(me + shift, sizes[axis])},
                device_id_type=pl.DeviceIdType.MESH,
            )
            total += 1
    pl.semaphore_wait(barrier, total)
    slot = 0
    pending, relays, local = [], [], []

    def remote(source, target, axis, peer, index):
        return pltpu.make_async_remote_copy(
            src_ref=source,
            dst_ref=target,
            send_sem=send_sem.at[index],
            recv_sem=recv_sem.at[index],
            device_id={axis: peer},
            device_id_type=pl.DeviceIdType.MESH,
        )

    for which, (kind, axis, span) in enumerate(plan):
        size = sizes[axis]
        me = lax.axis_index(axis)
        source, target = sources[which], targets[which]
        if kind == "relay":
            outer = size // 2
            column = lax.rem(me, 2)
            row = me // 2
            partner = row * 2 + 1 - column
            for shift in range(1, outer):
                peer = lax.rem(row + shift, outer) * 2 + column
                copy = remote(source, target.at[me], axis, peer, slot)
                copy.start()
                origin = lax.rem(row + outer - shift, outer) * 2 + column
                relays.append((copy, target, axis, origin, partner, slot + 1))
                slot += 2
            copy = remote(source, target.at[me], axis, partner, slot)
            copy.start()
            pending.append(copy)
            slot += 1
        else:
            for shift in range(1, size):
                peer = lax.rem(me + shift, size)
                piece = source if kind == "gather" else source.at[peer, :, span]
                copy = remote(piece, target.at[me], axis, peer, slot)
                copy.start()
                pending.append(copy)
                slot += 1
        piece = source if kind != "scatter" else source.at[me, :, span]
        copy = pltpu.make_async_copy(piece, target.at[me], own_sem.at[which])
        copy.start()
        local.append(copy)
    for copy, target, axis, origin, partner, index in relays:
        copy.wait_recv()
        onward = remote(target.at[origin], target.at[origin], axis, partner, index)
        onward.start()
        pending.append(onward)
    for copy, *_ in relays:
        copy.wait_send()
    for copy in pending + local:
        copy.wait()


def slots_of(kind, size):
    return 2 * (size // 2 - 1) + 1 if kind == "relay" else size - 1


def exchange(sizes, number, *ops):
    arrays = [op[2] for op in ops]
    spans = [slice(*op[3]) if len(op) > 3 else slice(0, op[2].shape[-1]) for op in ops]
    plan = tuple((op[0], op[1], span) for op, span in zip(ops, spans))
    shapes = [
        jax.ShapeDtypeStruct(
            array.shape[:-1] + (span.stop - span.start,)
            if kind == "scatter"
            else (sizes[axis],) + array.shape,
            array.dtype,
        )
        for (kind, axis, span), array in zip(plan, arrays)
    ]
    slots = sum(slots_of(kind, sizes[axis]) for kind, axis, _ in plan)
    return pl.pallas_call(
        functools.partial(exchange_kernel, plan, sizes),
        out_shape=shapes,
        in_specs=[pl.BlockSpec(memory_space=pltpu.VMEM)] * len(arrays),
        out_specs=[pl.BlockSpec(memory_space=pltpu.VMEM)] * len(arrays),
        scratch_shapes=[
            pltpu.SemaphoreType.DMA((len(arrays),)),
            pltpu.SemaphoreType.DMA((slots,)),
            pltpu.SemaphoreType.DMA((slots,)),
        ],
        compiler_params=pltpu.CompilerParams(
            collective_id=number, has_side_effects=True, vmem_limit_bytes=48 << 20
        ),
    )(*arrays)


def pad_columns(array, multiple=128):
    extra = -array.shape[-1] % multiple
    return jnp.pad(array, [(0, 0)] * (array.ndim - 1) + [(0, extra)])


def total_of(pieces):
    return jnp.sum(pieces.astype(jnp.float32), axis=0)


def dot_f32(left, right, left_dim, right_dim):
    return lax.dot_general(
        left, right, (((left_dim,), (right_dim,)), ((), ())), preferred_element_type=jnp.float32
    )


def feed_forward_kernel(
    hidden, rows_ref, up_ref, gate_ref, down_ref, cot_ref, mlp_ref, back_ref, grads_ref
):
    bf16 = jnp.bfloat16
    rows, cot = rows_ref[...], cot_ref[...]
    inputs = dot_f32(rows, up_ref[...], 1, 0)
    gate_part = dot_f32(rows, gate_ref[...], 1, 0)
    activated, gelu_slope = gelu_pair(inputs)
    hidden_act = (activated * gate_part).astype(bf16)
    mlp_ref[...] = dot_f32(hidden_act, down_ref[...], 1, 1).astype(bf16)
    grad_act = dot_f32(cot, down_ref[...], 1, 0)
    grad_up = (grad_act * gate_part * gelu_slope).astype(bf16)
    grad_gate = (grad_act * activated).astype(bf16)
    back_ref[...] = (
        dot_f32(grad_up, up_ref[...], 1, 1) + dot_f32(grad_gate, gate_ref[...], 1, 1)
    ).astype(bf16)
    grads_ref[:, :hidden] = dot_f32(rows, grad_up, 0, 0).astype(bf16)
    grads_ref[:, hidden : 2 * hidden] = dot_f32(rows, grad_gate, 0, 0).astype(bf16)
    grads_ref[:, 2 * hidden : 3 * hidden] = dot_f32(cot, hidden_act, 0, 0).astype(bf16)
    spare = grads_ref.shape[1] - 3 * hidden
    if spare:
        grads_ref[:, 3 * hidden :] = jnp.zeros((grads_ref.shape[0], spare), bf16)


def feed_forward(hidden, rows, up, gate, down_t, cot):
    row_count, width = rows.shape
    padded = -(-3 * hidden // 128) * 128
    return pl.pallas_call(
        functools.partial(feed_forward_kernel, hidden),
        out_shape=[
            jax.ShapeDtypeStruct((row_count, width), jnp.bfloat16),
            jax.ShapeDtypeStruct((row_count, width), jnp.bfloat16),
            jax.ShapeDtypeStruct((width, padded), jnp.bfloat16),
        ],
        in_specs=[pl.BlockSpec(memory_space=pltpu.VMEM)] * 5,
        out_specs=[pl.BlockSpec(memory_space=pltpu.VMEM)] * 3,
        compiler_params=pltpu.CompilerParams(vmem_limit_bytes=48 << 20),
    )(rows, up, gate, down_t, cot)


def body(sizes, tokens, attn_gain, w_qkv, w_out, mlp_gain, w_in, w_down, cotangent):
    bf16, f32 = jnp.bfloat16, jnp.float32
    groups, members = sizes["dp"], sizes["tensor"]
    block = w_qkv.shape[1]
    width = block * groups
    heads_wide, hidden = w_qkv.shape[2], w_in.shape[2]
    own_rows = tokens.shape[0]
    packed = pad_columns(
        jnp.concatenate(
            [w_qkv[0], w_qkv[1], w_qkv[2], w_out.T, w_in[0], w_in[1], w_down.T]
            + [attn_gain[:, None], mlp_gain[:, None]],
            axis=1,
        )
    )
    weights, token_rows, grad_rows = exchange(
        sizes,
        0,
        ("relay", "dp", packed),
        ("relay", "tensor", tokens),
        ("relay", "tensor", cotangent),
    )
    weights = weights.reshape(width, -1)
    edges = [3 * heads_wide, 4 * heads_wide, 4 * heads_wide + 2 * hidden, 4 * heads_wide + 3 * hidden]
    qkv_weight = weights[:, : edges[0]]
    out_weight_t = weights[:, edges[0] : edges[1]]
    in_weight = weights[:, edges[1] : edges[2]]
    down_weight_t = weights[:, edges[2] : edges[3]]
    gains = weights[:, edges[3] : edges[3] + 2].astype(f32).T
    attn_full, mlp_full = gains[0:1], gains[1:2]
    row_count = own_rows * members
    grad_rows = grad_rows.reshape(row_count, width)
    residual = tokens.astype(f32)
    normed_one, inv_one = normalize(residual)
    rows_one = (normalize(token_rows.reshape(row_count, width).astype(f32))[0] * attn_full).astype(bf16)
    head_count = heads_wide // HD
    head_shape = (row_count, head_count, HD)
    seq_shape = (row_count // L, L, head_count, HD)
    flat_shape = (row_count, heads_wide)
    cos_table, sin_table = rope_tables(row_count)
    projected = dot_f32(rows_one, qkv_weight, 1, 0)
    pieces = [projected[:, i * heads_wide : (i + 1) * heads_wide].reshape(head_shape) for i in range(3)]
    queries = rotate(pieces[0], cos_table, sin_table).astype(bf16).reshape(seq_shape)
    key_rows = rotate(pieces[1], cos_table, sin_table).astype(bf16).reshape(seq_shape)
    value_rows = pieces[2].astype(bf16).reshape(seq_shape)
    one_seq = row_count == L

    def over_sequences(function, arrays):
        if one_seq:
            results = function(*[array[0] for array in arrays])
            return tuple(result[None] for result in results)
        return lax.map(lambda seq_block: function(*seq_block), arrays)

    attn_mix, log_total = over_sequences(attend, (queries, key_rows, value_rows))
    mixed_rows = attn_mix.reshape(flat_shape)
    attn_part = dot_f32(mixed_rows, out_weight_t, 1, 1).astype(bf16)
    (attn_parts,) = exchange(
        sizes, 1, ("scatter", "tensor", attn_part.reshape(members, own_rows, width))
    )
    hidden_res = residual + total_of(attn_parts)
    normed_two, inv_two = normalize(hidden_res)
    ln_two = (normed_two * mlp_full).astype(bf16)
    (rows_two,) = exchange(sizes, 2, ("relay", "tensor", ln_two))
    rows_two = rows_two.reshape(row_count, width)
    mlp_part, ln_two_part, mlp_grads = feed_forward(
        hidden, rows_two, in_weight[:, :hidden], in_weight[:, hidden:], down_weight_t, grad_rows
    )
    mlp_grads = mlp_grads.reshape(groups, block, -1)
    mlp_wide = mlp_grads.shape[-1]
    first = mlp_wide // 384 * 128
    second = (mlp_wide - first) // 256 * 128 + first
    ln_two_parts, mlp_grads_a = exchange(
        sizes,
        3,
        ("scatter", "tensor", ln_two_part.reshape(members, own_rows, width)),
        ("scatter", "dp", mlp_grads, (0, first)),
    )
    grad_res_two, mlp_gain_part = normalize_back(total_of(ln_two_parts), normed_two, inv_two, mlp_full)
    grad_hidden = cotangent.astype(f32) + grad_res_two
    grad_hidden_rows, mlp_grads_b = exchange(
        sizes,
        4,
        ("relay", "tensor", grad_hidden.astype(bf16)),
        ("scatter", "dp", mlp_grads, (second, mlp_wide)),
    )
    grad_hidden_rows = grad_hidden_rows.reshape(row_count, width)
    grad_out_t = dot_f32(grad_hidden_rows, mixed_rows, 0, 0).astype(bf16)
    grad_mix = dot_f32(grad_hidden_rows, out_weight_t, 1, 0).astype(bf16).reshape(seq_shape)
    grad_q, grad_k, grad_v = over_sequences(
        attend_back, (queries, key_rows, value_rows, attn_mix, grad_mix, log_total)
    )
    grad_proj = jnp.concatenate(
        [
            rotate_back(grad_q.reshape(head_shape), cos_table, sin_table).reshape(flat_shape),
            rotate_back(grad_k.reshape(head_shape), cos_table, sin_table).reshape(flat_shape),
            grad_v.reshape(flat_shape),
        ],
        axis=1,
    ).astype(bf16)
    grad_qkv = dot_f32(rows_one, grad_proj, 0, 0).astype(bf16)
    ln_one_part = dot_f32(grad_proj, qkv_weight, 1, 1).astype(bf16)
    ln_one_parts, mlp_grads_c, grad_out_parts = exchange(
        sizes,
        5,
        ("scatter", "tensor", ln_one_part.reshape(members, own_rows, width)),
        ("scatter", "dp", mlp_grads, (first, second)),
        ("scatter", "dp", grad_out_t.reshape(groups, block, -1)),
    )
    grad_res_one, attn_gain_part = normalize_back(total_of(ln_one_parts), normed_one, inv_one, attn_full)
    input_grad = grad_hidden + grad_res_one
    gain_parts = jnp.stack([attn_gain_part, mlp_gain_part] + [jnp.zeros_like(attn_gain_part)] * 6)
    gain_parts = pad_columns(jnp.swapaxes(gain_parts.reshape(8, groups, block), 0, 1))
    late_parts, gain_parts, mlp_parts = exchange(
        sizes,
        6,
        ("scatter", "dp", grad_qkv.reshape(groups, block, -1)),
        ("scatter", "dp", gain_parts),
        ("scatter", "tensor", mlp_part.reshape(members, own_rows, width)),
    )
    output = (hidden_res + total_of(mlp_parts)).astype(bf16)
    (gain_groups,) = exchange(sizes, 7, ("gather", "tensor", total_of(gain_parts)))
    gain_sum = total_of(gain_groups)
    late = total_of(late_parts)
    grad_w_qkv = jnp.stack([late[:, i * heads_wide : (i + 1) * heads_wide] for i in range(3)])
    grad_w_out = total_of(grad_out_parts).T
    mlp_sums = jnp.concatenate(
        [total_of(mlp_grads_a), total_of(mlp_grads_c), total_of(mlp_grads_b)], axis=1
    )
    grad_w_in = jnp.stack([mlp_sums[:, :hidden], mlp_sums[:, hidden : 2 * hidden]])
    grad_w_down = mlp_sums[:, 2 * hidden : 3 * hidden].T
    return (
        output,
        input_grad,
        gain_sum[0, :block],
        grad_w_qkv,
        grad_w_out,
        gain_sum[1, :block],
        grad_w_in,
        grad_w_down,
    )


def solution(mesh):
    in_specs = (
        P(("dp", "tensor"), None),
        P("dp"),
        P(None, "dp", "tensor"),
        P("tensor", "dp"),
        P("dp"),
        P(None, "dp", "tensor"),
        P("tensor", "dp"),
        P(("dp", "tensor"), None),
    )
    out_specs = (
        P(("dp", "tensor"), None),
        P(("dp", "tensor"), None),
        P("dp"),
        P(None, "dp", "tensor"),
        P("tensor", "dp"),
        P("dp"),
        P(None, "dp", "tensor"),
        P("tensor", "dp"),
    )
    sizes = {axis: mesh.shape[axis] for axis in ("dp", "tensor")}
    return jax.shard_map(functools.partial(body, sizes), mesh=mesh, in_specs=in_specs, out_specs=out_specs, check_vma=False)
```

```python
import functools

import jax
import jax.numpy as jnp
from jax import lax
from jax.experimental import pallas as pl
from jax.experimental.pallas import tpu as pltpu
from jax.sharding import PartitionSpec as P

HD = 64
L = 512


NORM_EPS = 1e-05
ROPE_THETA = 160000.0
SQRT_HALF = 0.7071067811865476
GAUSS_NORM = 0.3989422804014327


def rope_tables(row_count):
    position = (jnp.arange(row_count) % L).astype(jnp.float32)
    halves = jnp.arange(HD // 2).astype(jnp.float32)
    inverse = ROPE_THETA ** (-2.0 * halves / HD)
    angles = position[:, None] * inverse[None, :]
    angles = jnp.concatenate([angles, angles], axis=1)
    return (jnp.cos(angles)[:, None, :], jnp.sin(angles)[:, None, :])


def rotate(field_rows, cos_table, sin_table):
    first_half = field_rows[..., : HD // 2]
    second_half = field_rows[..., HD // 2 :]
    turned = jnp.concatenate([-second_half, first_half], axis=-1)
    return field_rows * cos_table + turned * sin_table


def rotate_back(grad_field, cos_table, sin_table):
    scaled = grad_field * sin_table
    turned = jnp.concatenate([scaled[..., HD // 2 :], -scaled[..., : HD // 2]], axis=-1)
    return grad_field * cos_table + turned


def normalize(values):
    centred = values - jnp.mean(values, axis=-1, keepdims=True)
    inv_std = lax.rsqrt(jnp.mean(centred * centred, axis=-1, keepdims=True) + NORM_EPS)
    return (centred * inv_std, inv_std)


def normalize_back(grad_norm, normed, inv_std, gain_row):
    gain_part = jnp.sum(grad_norm * normed, axis=0)
    scaled = grad_norm * gain_row
    centred = scaled - jnp.mean(scaled, axis=-1, keepdims=True)
    grad_in = inv_std * (centred - normed * jnp.mean(scaled * normed, axis=-1, keepdims=True))
    return (grad_in, gain_part)


def gelu_pair(inputs):
    normal_cdf = 0.5 * (1.0 + lax.erf(inputs * SQRT_HALF))
    return (inputs * normal_cdf, normal_cdf + inputs * jnp.exp(-0.5 * inputs * inputs) * GAUSS_NORM)


def attend(queries, key_rows, value_rows):
    score_scale = HD ** (-0.5)
    scores = (
        jnp.einsum("qhd,khd->hqk", queries, key_rows, preferred_element_type=jnp.float32)
        * score_scale
    )
    row_max = jnp.max(scores, axis=-1, keepdims=True)
    log_total = row_max + jnp.log(jnp.sum(jnp.exp(scores - row_max), axis=-1, keepdims=True))
    weights = jnp.exp(scores - log_total).astype(jnp.bfloat16)
    attn_mix = jnp.einsum(
        "hqk,khd->qhd", weights, value_rows, preferred_element_type=jnp.float32
    ).astype(jnp.bfloat16)
    return (attn_mix, log_total)


def attend_back(queries, key_rows, value_rows, attn_mix, grad_mix, log_total):
    score_scale = HD ** (-0.5)
    scores = (
        jnp.einsum("qhd,khd->hqk", queries, key_rows, preferred_element_type=jnp.float32)
        * score_scale
    )
    probabilities = jnp.exp(scores - log_total)
    grad_probs = jnp.einsum(
        "qhd,khd->hqk", grad_mix, value_rows, preferred_element_type=jnp.float32
    )
    row_delta = jnp.sum(grad_mix.astype(jnp.float32) * attn_mix.astype(jnp.float32), axis=-1)
    grad_scores = (probabilities * (grad_probs - jnp.transpose(row_delta)[:, :, None])).astype(
        jnp.bfloat16
    )
    prob_rounded = probabilities.astype(jnp.bfloat16)
    grad_values = jnp.einsum(
        "hqk,qhd->khd", prob_rounded, grad_mix, preferred_element_type=jnp.float32
    )
    grad_queries = (
        jnp.einsum("hqk,khd->qhd", grad_scores, key_rows, preferred_element_type=jnp.float32)
        * score_scale
    )
    grad_keys = (
        jnp.einsum("hqk,qhd->khd", grad_scores, queries, preferred_element_type=jnp.float32)
        * score_scale
    )
    return (grad_queries, grad_keys, grad_values)


def exchange_kernel(plan, sizes, *refs):
    count = len(plan)
    sources, targets = refs[:count], refs[count : 2 * count]
    own_sem, send_sem, recv_sem = refs[2 * count :]
    axes = sorted({axis for _, axis, _ in plan})
    barrier = pltpu.get_barrier_semaphore()
    total = 0
    for axis in axes:
        me = lax.axis_index(axis)
        for shift in range(1, sizes[axis]):
            pl.semaphore_signal(
                barrier,
                inc=1,
                device_id={axis: lax.rem(me + shift, sizes[axis])},
                device_id_type=pl.DeviceIdType.MESH,
            )
            total += 1
    pl.semaphore_wait(barrier, total)
    slot = 0
    pending, relays, local = [], [], []

    def remote(source, target, axis, peer, index):
        return pltpu.make_async_remote_copy(
            src_ref=source,
            dst_ref=target,
            send_sem=send_sem.at[index],
            recv_sem=recv_sem.at[index],
            device_id={axis: peer},
            device_id_type=pl.DeviceIdType.MESH,
        )

    for which, (kind, axis, span) in enumerate(plan):
        size = sizes[axis]
        me = lax.axis_index(axis)
        source, target = sources[which], targets[which]
        outer = size // 2
        column = lax.rem(me, 2)
        row = me // 2
        partner = row * 2 + 1 - column
        if kind == "half":
            copy = remote(source.at[:, 1 - column, :, span], target, axis, partner, slot)
            copy.start()
            pending.append(copy)
            slot += 1
            continue
        if kind == "outer":
            for shift in range(1, outer):
                other = lax.rem(row + shift, outer)
                copy = remote(source.at[other], target.at[row], axis, other * 2 + column, slot)
                copy.start()
                pending.append(copy)
                slot += 1
            copy = pltpu.make_async_copy(source.at[row], target.at[row], own_sem.at[which])
            copy.start()
            local.append(copy)
            continue
        if kind == "relay":
            for shift in range(1, outer):
                peer = lax.rem(row + shift, outer) * 2 + column
                copy = remote(source, target.at[me], axis, peer, slot)
                copy.start()
                origin = lax.rem(row + outer - shift, outer) * 2 + column
                relays.append((copy, target, axis, origin, partner, slot + 1))
                slot += 2
            copy = remote(source, target.at[me], axis, partner, slot)
            copy.start()
            pending.append(copy)
            slot += 1
        else:
            for shift in range(1, size):
                peer = lax.rem(me + shift, size)
                piece = source if kind == "gather" else source.at[peer, :, span]
                copy = remote(piece, target.at[me], axis, peer, slot)
                copy.start()
                pending.append(copy)
                slot += 1
        piece = source if kind != "scatter" else source.at[me, :, span]
        copy = pltpu.make_async_copy(piece, target.at[me], own_sem.at[which])
        copy.start()
        local.append(copy)
    for copy, target, axis, origin, partner, index in relays:
        copy.wait_recv()
        onward = remote(target.at[origin], target.at[origin], axis, partner, index)
        onward.start()
        pending.append(onward)
    for copy, *_ in relays:
        copy.wait_send()
    for copy in pending + local:
        copy.wait()


def slots_of(kind, size):
    outer = size // 2
    return {"relay": 2 * outer - 1, "half": 1, "outer": outer - 1}.get(kind, size - 1)


def shape_of(kind, size, shape, wide):
    if kind == "half":
        return (shape[0], shape[2], wide)
    return {"scatter": shape[:-1] + (wide,), "outer": shape}.get(kind, (size,) + shape)


def exchange(sizes, number, *ops):
    arrays = [op[2] for op in ops]
    spans = [slice(*op[3]) if len(op) > 3 else slice(0, op[2].shape[-1]) for op in ops]
    plan = tuple((op[0], op[1], span) for op, span in zip(ops, spans))
    shapes = [
        jax.ShapeDtypeStruct(
            shape_of(kind, sizes[axis], array.shape, span.stop - span.start), array.dtype
        )
        for (kind, axis, span), array in zip(plan, arrays)
    ]
    slots = sum(slots_of(kind, sizes[axis]) for kind, axis, _ in plan)
    return pl.pallas_call(
        functools.partial(exchange_kernel, plan, sizes),
        out_shape=shapes,
        in_specs=[pl.BlockSpec(memory_space=pltpu.VMEM)] * len(arrays),
        out_specs=[pl.BlockSpec(memory_space=pltpu.VMEM)] * len(arrays),
        scratch_shapes=[
            pltpu.SemaphoreType.DMA((len(arrays),)),
            pltpu.SemaphoreType.DMA((slots,)),
            pltpu.SemaphoreType.DMA((slots,)),
        ],
        compiler_params=pltpu.CompilerParams(
            collective_id=number, has_side_effects=True, vmem_limit_bytes=48 << 20
        ),
    )(*arrays)


def pad_columns(array, multiple=128):
    extra = -array.shape[-1] % multiple
    return jnp.pad(array, [(0, 0)] * (array.ndim - 1) + [(0, extra)])


def total_of(pieces):
    return jnp.sum(pieces.astype(jnp.float32), axis=0)


def dot_f32(left, right, left_dim, right_dim):
    return lax.dot_general(
        left, right, (((left_dim,), (right_dim,)), ((), ())), preferred_element_type=jnp.float32
    )


def feed_forward_kernel(
    hidden, rows_ref, up_ref, gate_ref, down_ref, cot_ref, mlp_ref, back_ref, grads_ref
):
    bf16 = jnp.bfloat16
    rows, cot = rows_ref[...], cot_ref[...]
    inputs = dot_f32(rows, up_ref[...], 1, 0)
    gate_part = dot_f32(rows, gate_ref[...], 1, 0)
    activated, gelu_slope = gelu_pair(inputs)
    hidden_act = (activated * gate_part).astype(bf16)
    mlp_ref[...] = dot_f32(hidden_act, down_ref[...], 1, 1).astype(bf16)
    grad_act = dot_f32(cot, down_ref[...], 1, 0)
    grad_up = (grad_act * gate_part * gelu_slope).astype(bf16)
    grad_gate = (grad_act * activated).astype(bf16)
    back_ref[...] = (
        dot_f32(grad_up, up_ref[...], 1, 1) + dot_f32(grad_gate, gate_ref[...], 1, 1)
    ).astype(bf16)
    grads_ref[:, :hidden] = dot_f32(rows, grad_up, 0, 0).astype(bf16)
    grads_ref[:, hidden : 2 * hidden] = dot_f32(rows, grad_gate, 0, 0).astype(bf16)
    grads_ref[:, 2 * hidden : 3 * hidden] = dot_f32(cot, hidden_act, 0, 0).astype(bf16)
    spare = grads_ref.shape[1] - 3 * hidden
    if spare:
        grads_ref[:, 3 * hidden :] = jnp.zeros((grads_ref.shape[0], spare), bf16)


def feed_forward(hidden, rows, up, gate, down_t, cot):
    row_count, width = rows.shape
    padded = -(-3 * hidden // 128) * 128
    return pl.pallas_call(
        functools.partial(feed_forward_kernel, hidden),
        out_shape=[
            jax.ShapeDtypeStruct((row_count, width), jnp.bfloat16),
            jax.ShapeDtypeStruct((row_count, width), jnp.bfloat16),
            jax.ShapeDtypeStruct((width, padded), jnp.bfloat16),
        ],
        in_specs=[pl.BlockSpec(memory_space=pltpu.VMEM)] * 5,
        out_specs=[pl.BlockSpec(memory_space=pltpu.VMEM)] * 3,
        compiler_params=pltpu.CompilerParams(vmem_limit_bytes=48 << 20),
    )(rows, up, gate, down_t, cot)


def body(sizes, tokens, attn_gain, w_qkv, w_out, mlp_gain, w_in, w_down, cotangent):
    bf16, f32 = jnp.bfloat16, jnp.float32
    groups, members = sizes["dp"], sizes["tensor"]
    block = w_qkv.shape[1]
    width = block * groups
    heads_wide, hidden = w_qkv.shape[2], w_in.shape[2]
    own_rows = tokens.shape[0]
    packed = jnp.concatenate([w_qkv[0], w_qkv[1], w_qkv[2], w_out.T], axis=1)
    gain_tile = jnp.pad(jnp.stack([attn_gain, mlp_gain]), [(0, 14), (0, -block % 128)])
    weights, gain_tiles, token_rows, grad_rows = exchange(
        sizes,
        0,
        ("relay", "dp", packed),
        ("relay", "dp", gain_tile),
        ("relay", "tensor", tokens),
        ("relay", "tensor", cotangent),
    )
    weights = weights.reshape(width, -1)
    qkv_weight = weights[:, : 3 * heads_wide]
    out_weight_t = weights[:, 3 * heads_wide :]
    attn_full = gain_tiles[:, 0, :block].reshape(1, width).astype(f32)
    mlp_full = gain_tiles[:, 1, :block].reshape(1, width).astype(f32)
    outer = groups // 2
    column = lax.rem(lax.axis_index("dp"), 2)

    def quarter(array):
        return array.reshape(outer, 2, block, -1)

    def half_sum(array, received, low, high):
        own = lax.dynamic_index_in_dim(quarter(array)[..., low:high], column, 1, keepdims=False)
        return (own.astype(f32) + received.astype(f32)).astype(bf16)

    row_count = own_rows * members
    grad_rows = grad_rows.reshape(row_count, width)
    residual = tokens.astype(f32)
    normed_one, inv_one = normalize(residual)
    rows_one = (normalize(token_rows.reshape(row_count, width).astype(f32))[0] * attn_full).astype(bf16)
    head_count = heads_wide // HD
    head_shape = (row_count, head_count, HD)
    seq_shape = (row_count // L, L, head_count, HD)
    flat_shape = (row_count, heads_wide)
    cos_table, sin_table = rope_tables(row_count)
    projected = dot_f32(rows_one, qkv_weight, 1, 0)
    pieces = [projected[:, i * heads_wide : (i + 1) * heads_wide].reshape(head_shape) for i in range(3)]
    queries = rotate(pieces[0], cos_table, sin_table).astype(bf16).reshape(seq_shape)
    key_rows = rotate(pieces[1], cos_table, sin_table).astype(bf16).reshape(seq_shape)
    value_rows = pieces[2].astype(bf16).reshape(seq_shape)
    one_seq = row_count == L

    def over_sequences(function, arrays):
        if one_seq:
            results = function(*[array[0] for array in arrays])
            return tuple(result[None] for result in results)
        return lax.map(lambda seq_block: function(*seq_block), arrays)

    attn_mix, log_total = over_sequences(attend, (queries, key_rows, value_rows))
    mixed_rows = attn_mix.reshape(flat_shape)
    attn_part = dot_f32(mixed_rows, out_weight_t, 1, 1).astype(bf16)
    attn_parts, up_weight, down_weight_t = exchange(
        sizes,
        1,
        ("scatter", "tensor", attn_part.reshape(members, own_rows, width)),
        ("relay", "dp", w_in[0]),
        ("relay", "dp", w_down.T),
    )
    up_weight = up_weight.reshape(width, -1)
    down_weight_t = down_weight_t.reshape(width, -1)
    hidden_res = residual + total_of(attn_parts)
    normed_two, inv_two = normalize(hidden_res)
    ln_two = (normed_two * mlp_full).astype(bf16)
    rows_two, gate_weight = exchange(
        sizes, 2, ("relay", "tensor", ln_two), ("relay", "dp", w_in[1])
    )
    gate_weight = gate_weight.reshape(width, -1)
    rows_two = rows_two.reshape(row_count, width)
    mlp_part, ln_two_part, mlp_grads = feed_forward(
        hidden, rows_two, up_weight, gate_weight, down_weight_t, grad_rows
    )
    mlp_wide = mlp_grads.shape[-1]
    first = mlp_wide // 256 * 128
    ln_two_parts, mlp_grads_a = exchange(
        sizes,
        3,
        ("scatter", "tensor", ln_two_part.reshape(members, own_rows, width)),
        ("half", "dp", quarter(mlp_grads), (0, first)),
    )
    grad_res_two, mlp_gain_part = normalize_back(total_of(ln_two_parts), normed_two, inv_two, mlp_full)
    grad_hidden = cotangent.astype(f32) + grad_res_two
    grad_hidden_rows, mlp_grads_b, mlp_sums_a = exchange(
        sizes,
        4,
        ("relay", "tensor", grad_hidden.astype(bf16)),
        ("half", "dp", quarter(mlp_grads), (first, mlp_wide)),
        ("outer", "dp", half_sum(mlp_grads, mlp_grads_a, 0, first)),
    )
    grad_hidden_rows = grad_hidden_rows.reshape(row_count, width)
    grad_out_t = dot_f32(grad_hidden_rows, mixed_rows, 0, 0).astype(bf16)
    grad_mix = dot_f32(grad_hidden_rows, out_weight_t, 1, 0).astype(bf16).reshape(seq_shape)
    grad_q, grad_k, grad_v = over_sequences(
        attend_back, (queries, key_rows, value_rows, attn_mix, grad_mix, log_total)
    )
    grad_proj = jnp.concatenate(
        [
            rotate_back(grad_q.reshape(head_shape), cos_table, sin_table).reshape(flat_shape),
            rotate_back(grad_k.reshape(head_shape), cos_table, sin_table).reshape(flat_shape),
            grad_v.reshape(flat_shape),
        ],
        axis=1,
    ).astype(bf16)
    grad_qkv = dot_f32(rows_one, grad_proj, 0, 0).astype(bf16)
    ln_one_part = dot_f32(grad_proj, qkv_weight, 1, 1).astype(bf16)
    ln_one_parts, mlp_sums_b, grad_out_half = exchange(
        sizes,
        5,
        ("scatter", "tensor", ln_one_part.reshape(members, own_rows, width)),
        ("outer", "dp", half_sum(mlp_grads, mlp_grads_b, first, mlp_wide)),
        ("half", "dp", quarter(grad_out_t)),
    )
    grad_res_one, attn_gain_part = normalize_back(total_of(ln_one_parts), normed_one, inv_one, attn_full)
    input_grad = grad_hidden + grad_res_one
    gain_parts = jnp.stack([attn_gain_part, mlp_gain_part] + [jnp.zeros_like(attn_gain_part)] * 6)
    gain_parts = pad_columns(jnp.swapaxes(gain_parts.reshape(8, groups, block), 0, 1))
    qkv_half, gain_parts, mlp_parts, grad_out_parts = exchange(
        sizes,
        6,
        ("half", "dp", quarter(grad_qkv)),
        ("scatter", "dp", gain_parts),
        ("scatter", "tensor", mlp_part.reshape(members, own_rows, width)),
        ("outer", "dp", half_sum(grad_out_t, grad_out_half, 0, heads_wide)),
    )
    output = (hidden_res + total_of(mlp_parts)).astype(bf16)
    gain_groups, late_parts = exchange(
        sizes,
        7,
        ("gather", "tensor", total_of(gain_parts)),
        ("outer", "dp", half_sum(grad_qkv, qkv_half, 0, 3 * heads_wide)),
    )
    gain_sum = total_of(gain_groups)
    late = total_of(late_parts)
    grad_w_qkv = jnp.stack([late[:, i * heads_wide : (i + 1) * heads_wide] for i in range(3)])
    grad_w_out = total_of(grad_out_parts).T
    mlp_sums = jnp.concatenate(
        [total_of(mlp_sums_a), total_of(mlp_sums_b)], axis=1
    )
    grad_w_in = jnp.stack([mlp_sums[:, :hidden], mlp_sums[:, hidden : 2 * hidden]])
    grad_w_down = mlp_sums[:, 2 * hidden : 3 * hidden].T
    return (
        output,
        input_grad,
        gain_sum[0, :block],
        grad_w_qkv,
        grad_w_out,
        gain_sum[1, :block],
        grad_w_in,
        grad_w_down,
    )


def solution(mesh):
    in_specs = (
        P(("dp", "tensor"), None),
        P("dp"),
        P(None, "dp", "tensor"),
        P("tensor", "dp"),
        P("dp"),
        P(None, "dp", "tensor"),
        P("tensor", "dp"),
        P(("dp", "tensor"), None),
    )
    out_specs = (
        P(("dp", "tensor"), None),
        P(("dp", "tensor"), None),
        P("dp"),
        P(None, "dp", "tensor"),
        P("tensor", "dp"),
        P("dp"),
        P(None, "dp", "tensor"),
        P("tensor", "dp"),
    )
    sizes = {axis: mesh.shape[axis] for axis in ("dp", "tensor")}
    return jax.shard_map(functools.partial(body, sizes), mesh=mesh, in_specs=in_specs, out_specs=out_specs, check_vma=False)
```

```python
import functools

import jax
import jax.numpy as jnp
from jax import lax
from jax.experimental import pallas as pl
from jax.experimental.pallas import tpu as pltpu
from jax.experimental.layout import Layout, with_layout_constraint
from jax.sharding import PartitionSpec as P

HD = 64
L = 512


NORM_EPS = 1e-05
ROPE_THETA = 160000.0
SQRT_HALF = 0.7071067811865476
GAUSS_NORM = 0.3989422804014327


def rope_tables(row_count):
    position = (jnp.arange(row_count) % L).astype(jnp.float32)
    halves = jnp.arange(HD // 2).astype(jnp.float32)
    inverse = ROPE_THETA ** (-2.0 * halves / HD)
    angles = position[:, None] * inverse[None, :]
    angles = jnp.concatenate([angles, angles], axis=1)
    return (jnp.cos(angles)[:, None, :], jnp.sin(angles)[:, None, :])


def rotate(field_rows, cos_table, sin_table):
    first_half = field_rows[..., : HD // 2]
    second_half = field_rows[..., HD // 2 :]
    turned = jnp.concatenate([-second_half, first_half], axis=-1)
    return field_rows * cos_table + turned * sin_table


def rotate_back(grad_field, cos_table, sin_table):
    scaled = grad_field * sin_table
    turned = jnp.concatenate([scaled[..., HD // 2 :], -scaled[..., : HD // 2]], axis=-1)
    return grad_field * cos_table + turned


def normalize(values):
    centred = values - jnp.mean(values, axis=-1, keepdims=True)
    inv_std = lax.rsqrt(jnp.mean(centred * centred, axis=-1, keepdims=True) + NORM_EPS)
    return (centred * inv_std, inv_std)


def normalize_back(grad_norm, normed, inv_std, gain_row):
    gain_part = jnp.sum(grad_norm * normed, axis=0)
    scaled = grad_norm * gain_row
    centred = scaled - jnp.mean(scaled, axis=-1, keepdims=True)
    grad_in = inv_std * (centred - normed * jnp.mean(scaled * normed, axis=-1, keepdims=True))
    return (grad_in, gain_part)


def gelu_pair(inputs):
    normal_cdf = 0.5 * (1.0 + lax.erf(inputs * SQRT_HALF))
    return (inputs * normal_cdf, normal_cdf + inputs * jnp.exp(-0.5 * inputs * inputs) * GAUSS_NORM)


def attend(queries, key_rows, value_rows):
    score_scale = HD ** (-0.5)
    scores = (
        jnp.einsum("qhd,khd->hqk", queries, key_rows, preferred_element_type=jnp.float32)
        * score_scale
    )
    row_max = jnp.max(scores, axis=-1, keepdims=True)
    log_total = row_max + jnp.log(jnp.sum(jnp.exp(scores - row_max), axis=-1, keepdims=True))
    weights = jnp.exp(scores - log_total).astype(jnp.bfloat16)
    attn_mix = jnp.einsum(
        "hqk,khd->qhd", weights, value_rows, preferred_element_type=jnp.float32
    ).astype(jnp.bfloat16)
    return (attn_mix, log_total)


def attend_back(queries, key_rows, value_rows, attn_mix, grad_mix, log_total):
    score_scale = HD ** (-0.5)
    scores = (
        jnp.einsum("qhd,khd->hqk", queries, key_rows, preferred_element_type=jnp.float32)
        * score_scale
    )
    probabilities = jnp.exp(scores - log_total)
    grad_probs = jnp.einsum(
        "qhd,khd->hqk", grad_mix, value_rows, preferred_element_type=jnp.float32
    )
    row_delta = jnp.sum(grad_mix.astype(jnp.float32) * attn_mix.astype(jnp.float32), axis=-1)
    grad_scores = (probabilities * (grad_probs - jnp.transpose(row_delta)[:, :, None])).astype(
        jnp.bfloat16
    )
    prob_rounded = probabilities.astype(jnp.bfloat16)
    grad_values = jnp.einsum(
        "hqk,qhd->khd", prob_rounded, grad_mix, preferred_element_type=jnp.float32
    )
    grad_queries = (
        jnp.einsum("hqk,khd->qhd", grad_scores, key_rows, preferred_element_type=jnp.float32)
        * score_scale
    )
    grad_keys = (
        jnp.einsum("hqk,qhd->khd", grad_scores, queries, preferred_element_type=jnp.float32)
        * score_scale
    )
    return (grad_queries, grad_keys, grad_values)


def exchange_kernel(plan, sizes, *refs):
    count = len(plan)
    sources, targets = refs[:count], refs[count : 2 * count]
    own_sem, send_sem, recv_sem = refs[2 * count :]
    axes = sorted({axis for _, axis, _ in plan})
    barrier = pltpu.get_barrier_semaphore()
    total = 0
    for axis in axes:
        me = lax.axis_index(axis)
        for shift in range(1, sizes[axis]):
            pl.semaphore_signal(
                barrier,
                inc=1,
                device_id={axis: lax.rem(me + shift, sizes[axis])},
                device_id_type=pl.DeviceIdType.MESH,
            )
            total += 1
    pl.semaphore_wait(barrier, total)
    slot = 0
    pending, relays, local = [], [], []

    def remote(source, target, axis, peer, index):
        return pltpu.make_async_remote_copy(
            src_ref=source,
            dst_ref=target,
            send_sem=send_sem.at[index],
            recv_sem=recv_sem.at[index],
            device_id={axis: peer},
            device_id_type=pl.DeviceIdType.MESH,
        )

    for which, (kind, axis, span) in enumerate(plan):
        size = sizes[axis]
        me = lax.axis_index(axis)
        source, target = sources[which], targets[which]
        outer = size // 2
        column = lax.rem(me, 2)
        row = me // 2
        partner = row * 2 + 1 - column
        if kind == "half":
            copy = remote(source.at[:, 1 - column, :, span], target, axis, partner, slot)
            copy.start()
            pending.append(copy)
            slot += 1
            continue
        if kind == "outer":
            for shift in range(1, outer):
                other = lax.rem(row + shift, outer)
                copy = remote(source.at[other], target.at[row], axis, other * 2 + column, slot)
                copy.start()
                pending.append(copy)
                slot += 1
            copy = pltpu.make_async_copy(source.at[row], target.at[row], own_sem.at[which])
            copy.start()
            local.append(copy)
            continue
        if kind == "relay":
            for shift in range(1, outer):
                peer = lax.rem(row + shift, outer) * 2 + column
                copy = remote(source, target.at[me], axis, peer, slot)
                copy.start()
                origin = lax.rem(row + outer - shift, outer) * 2 + column
                relays.append((copy, target, axis, origin, partner, slot + 1))
                slot += 2
            copy = remote(source, target.at[me], axis, partner, slot)
            copy.start()
            pending.append(copy)
            slot += 1
        else:
            for shift in range(1, size):
                peer = lax.rem(me + shift, size)
                piece = source if kind == "gather" else source.at[peer, :, span]
                copy = remote(piece, target.at[me], axis, peer, slot)
                copy.start()
                pending.append(copy)
                slot += 1
        piece = source if kind != "scatter" else source.at[me, :, span]
        copy = pltpu.make_async_copy(piece, target.at[me], own_sem.at[which])
        copy.start()
        local.append(copy)
    for copy, target, axis, origin, partner, index in relays:
        copy.wait_recv()
        onward = remote(target.at[origin], target.at[origin], axis, partner, index)
        onward.start()
        pending.append(onward)
    for copy, *_ in relays:
        copy.wait_send()
    for copy in pending + local:
        copy.wait()


def slots_of(kind, size):
    outer = size // 2
    return {"relay": 2 * outer - 1, "half": 1, "outer": outer - 1}.get(kind, size - 1)


def shape_of(kind, size, shape, wide):
    if kind == "half":
        return (shape[0], shape[2], wide)
    return {"scatter": shape[:-1] + (wide,), "outer": shape}.get(kind, (size,) + shape)


def exchange(sizes, number, *ops):
    arrays = [op[2] for op in ops]
    spans = [slice(*op[3]) if len(op) > 3 else slice(0, op[2].shape[-1]) for op in ops]
    plan = tuple((op[0], op[1], span) for op, span in zip(ops, spans))
    shapes = [
        jax.ShapeDtypeStruct(
            shape_of(kind, sizes[axis], array.shape, span.stop - span.start), array.dtype
        )
        for (kind, axis, span), array in zip(plan, arrays)
    ]
    slots = sum(slots_of(kind, sizes[axis]) for kind, axis, _ in plan)
    return pl.pallas_call(
        functools.partial(exchange_kernel, plan, sizes),
        out_shape=shapes,
        in_specs=[pl.BlockSpec(memory_space=pltpu.VMEM)] * len(arrays),
        out_specs=[pl.BlockSpec(memory_space=pltpu.VMEM)] * len(arrays),
        scratch_shapes=[
            pltpu.SemaphoreType.DMA((len(arrays),)),
            pltpu.SemaphoreType.DMA((slots,)),
            pltpu.SemaphoreType.DMA((slots,)),
        ],
        compiler_params=pltpu.CompilerParams(
            collective_id=number, has_side_effects=True, vmem_limit_bytes=48 << 20
        ),
    )(*arrays)


def pad_columns(array, multiple=128):
    extra = -array.shape[-1] % multiple
    return jnp.pad(array, [(0, 0)] * (array.ndim - 1) + [(0, extra)])


def total_of(pieces):
    return jnp.sum(pieces.astype(jnp.float32), axis=0)


def row_major(array):
    return with_layout_constraint(array, Layout(major_to_minor=(0, 1)))


def dot_f32(left, right, left_dim, right_dim):
    return lax.dot_general(
        left, right, (((left_dim,), (right_dim,)), ((), ())), preferred_element_type=jnp.float32
    )


def feed_forward_kernel(
    hidden, rows_ref, up_ref, gate_ref, down_ref, cot_ref, mlp_ref, back_ref, grads_ref
):
    bf16 = jnp.bfloat16
    rows, cot = rows_ref[...], cot_ref[...]
    inputs = dot_f32(rows, up_ref[...], 1, 0)
    gate_part = dot_f32(rows, gate_ref[...], 1, 0)
    activated, gelu_slope = gelu_pair(inputs)
    hidden_act = (activated * gate_part).astype(bf16)
    mlp_ref[...] = dot_f32(hidden_act, down_ref[...], 1, 1).astype(bf16)
    grad_act = dot_f32(cot, down_ref[...], 1, 0)
    grad_up = (grad_act * gate_part * gelu_slope).astype(bf16)
    grad_gate = (grad_act * activated).astype(bf16)
    back_ref[...] = (
        dot_f32(grad_up, up_ref[...], 1, 1) + dot_f32(grad_gate, gate_ref[...], 1, 1)
    ).astype(bf16)
    grads_ref[:, :hidden] = dot_f32(rows, grad_up, 0, 0).astype(bf16)
    grads_ref[:, hidden : 2 * hidden] = dot_f32(rows, grad_gate, 0, 0).astype(bf16)
    grads_ref[:, 2 * hidden : 3 * hidden] = dot_f32(cot, hidden_act, 0, 0).astype(bf16)
    spare = grads_ref.shape[1] - 3 * hidden
    if spare:
        grads_ref[:, 3 * hidden :] = jnp.zeros((grads_ref.shape[0], spare), bf16)


def feed_forward(hidden, rows, up, gate, down_t, cot):
    row_count, width = rows.shape
    padded = -(-3 * hidden // 128) * 128
    return pl.pallas_call(
        functools.partial(feed_forward_kernel, hidden),
        out_shape=[
            jax.ShapeDtypeStruct((row_count, width), jnp.bfloat16),
            jax.ShapeDtypeStruct((row_count, width), jnp.bfloat16),
            jax.ShapeDtypeStruct((width, padded), jnp.bfloat16),
        ],
        in_specs=[pl.BlockSpec(memory_space=pltpu.VMEM)] * 5,
        out_specs=[pl.BlockSpec(memory_space=pltpu.VMEM)] * 3,
        compiler_params=pltpu.CompilerParams(vmem_limit_bytes=48 << 20),
    )(rows, up, gate, down_t, cot)


def body(sizes, tokens, attn_gain, w_qkv, w_out, mlp_gain, w_in, w_down, cotangent):
    bf16, f32 = jnp.bfloat16, jnp.float32
    groups, members = sizes["dp"], sizes["tensor"]
    block = w_qkv.shape[1]
    width = block * groups
    heads_wide, hidden = w_qkv.shape[2], w_in.shape[2]
    own_rows = tokens.shape[0]
    packed = jnp.concatenate([w_qkv[0], w_qkv[1], w_qkv[2], w_out.T], axis=1)
    gain_tile = jnp.pad(jnp.stack([attn_gain, mlp_gain]), [(0, 14), (0, -block % 128)])
    weights, gain_tiles, token_rows, grad_rows = exchange(
        sizes,
        0,
        ("relay", "dp", packed),
        ("relay", "dp", gain_tile),
        ("relay", "tensor", tokens),
        ("relay", "tensor", cotangent),
    )
    weights = weights.reshape(width, -1)
    qkv_weight = weights[:, : 3 * heads_wide]
    out_weight_t = weights[:, 3 * heads_wide :]
    attn_full = gain_tiles[:, 0, :block].reshape(1, width).astype(f32)
    mlp_full = gain_tiles[:, 1, :block].reshape(1, width).astype(f32)
    outer = groups // 2
    column = lax.rem(lax.axis_index("dp"), 2)

    def quarter(array):
        return array.reshape(outer, 2, block, -1)

    def half_sum(array, received, low, high):
        own = lax.dynamic_index_in_dim(quarter(array)[..., low:high], column, 1, keepdims=False)
        return (own.astype(f32) + received.astype(f32)).astype(bf16)

    row_count = own_rows * members
    grad_rows = grad_rows.reshape(row_count, width)
    residual = tokens.astype(f32)
    normed_one, inv_one = normalize(residual)
    rows_one = (normalize(token_rows.reshape(row_count, width).astype(f32))[0] * attn_full).astype(bf16)
    head_count = heads_wide // HD
    head_shape = (row_count, head_count, HD)
    seq_shape = (row_count // L, L, head_count, HD)
    flat_shape = (row_count, heads_wide)
    cos_table, sin_table = rope_tables(row_count)
    projected = dot_f32(rows_one, qkv_weight, 1, 0)
    pieces = [projected[:, i * heads_wide : (i + 1) * heads_wide].reshape(head_shape) for i in range(3)]
    queries = rotate(pieces[0], cos_table, sin_table).astype(bf16).reshape(seq_shape)
    key_rows = rotate(pieces[1], cos_table, sin_table).astype(bf16).reshape(seq_shape)
    value_rows = pieces[2].astype(bf16).reshape(seq_shape)
    one_seq = row_count == L

    def over_sequences(function, arrays):
        if one_seq:
            results = function(*[array[0] for array in arrays])
            return tuple(result[None] for result in results)
        return lax.map(lambda seq_block: function(*seq_block), arrays)

    attn_mix, log_total = over_sequences(attend, (queries, key_rows, value_rows))
    mixed_rows = attn_mix.reshape(flat_shape)
    attn_part = dot_f32(mixed_rows, out_weight_t, 1, 1).astype(bf16)
    attn_parts, up_weight, down_weight_t = exchange(
        sizes,
        1,
        ("scatter", "tensor", attn_part.reshape(members, own_rows, width)),
        ("relay", "dp", w_in[0]),
        ("relay", "dp", w_down.T),
    )
    up_weight = up_weight.reshape(width, -1)
    down_weight_t = down_weight_t.reshape(width, -1)
    hidden_res = residual + total_of(attn_parts)
    normed_two, inv_two = normalize(hidden_res)
    ln_two = (normed_two * mlp_full).astype(bf16)
    rows_two, gate_weight = exchange(
        sizes, 2, ("relay", "tensor", ln_two), ("relay", "dp", w_in[1])
    )
    gate_weight = gate_weight.reshape(width, -1)
    rows_two = rows_two.reshape(row_count, width)
    mlp_part, ln_two_part, mlp_grads = feed_forward(
        hidden, rows_two, up_weight, gate_weight, down_weight_t, grad_rows
    )
    mlp_wide = mlp_grads.shape[-1]
    first = mlp_wide // 256 * 128
    ln_two_parts, mlp_grads_a = exchange(
        sizes,
        3,
        ("scatter", "tensor", ln_two_part.reshape(members, own_rows, width)),
        ("half", "dp", quarter(mlp_grads), (0, first)),
    )
    grad_res_two, mlp_gain_part = normalize_back(total_of(ln_two_parts), normed_two, inv_two, mlp_full)
    grad_hidden = cotangent.astype(f32) + grad_res_two
    grad_hidden_rows, mlp_grads_b, mlp_sums_a = exchange(
        sizes,
        4,
        ("relay", "tensor", grad_hidden.astype(bf16)),
        ("half", "dp", quarter(mlp_grads), (first, mlp_wide)),
        ("outer", "dp", half_sum(mlp_grads, mlp_grads_a, 0, first)),
    )
    grad_hidden_rows = grad_hidden_rows.reshape(row_count, width)
    grad_out_t = row_major(dot_f32(grad_hidden_rows, mixed_rows, 0, 0).astype(bf16))
    grad_mix = dot_f32(grad_hidden_rows, out_weight_t, 1, 0).astype(bf16).reshape(seq_shape)
    grad_q, grad_k, grad_v = over_sequences(
        attend_back, (queries, key_rows, value_rows, attn_mix, grad_mix, log_total)
    )
    grad_proj = jnp.concatenate(
        [
            rotate_back(grad_q.reshape(head_shape), cos_table, sin_table).reshape(flat_shape),
            rotate_back(grad_k.reshape(head_shape), cos_table, sin_table).reshape(flat_shape),
            grad_v.reshape(flat_shape),
        ],
        axis=1,
    ).astype(bf16)
    grad_qkv = row_major(dot_f32(rows_one, grad_proj, 0, 0).astype(bf16))
    ln_one_part = dot_f32(grad_proj, qkv_weight, 1, 1).astype(bf16)
    ln_one_parts, mlp_sums_b, grad_out_half, qkv_half = exchange(
        sizes,
        5,
        ("scatter", "tensor", ln_one_part.reshape(members, own_rows, width)),
        ("outer", "dp", half_sum(mlp_grads, mlp_grads_b, first, mlp_wide)),
        ("half", "dp", quarter(grad_out_t)),
        ("half", "dp", quarter(grad_qkv)),
    )
    grad_res_one, attn_gain_part = normalize_back(total_of(ln_one_parts), normed_one, inv_one, attn_full)
    input_grad = grad_hidden + grad_res_one
    gain_parts = jnp.stack([attn_gain_part, mlp_gain_part] + [jnp.zeros_like(attn_gain_part)] * 6)
    gain_parts = pad_columns(jnp.swapaxes(gain_parts.reshape(8, groups, block), 0, 1))
    late_parts, gain_parts, mlp_parts, grad_out_parts = exchange(
        sizes,
        6,
        ("outer", "dp", half_sum(grad_qkv, qkv_half, 0, 3 * heads_wide)),
        ("scatter", "dp", gain_parts),
        ("scatter", "tensor", mlp_part.reshape(members, own_rows, width)),
        ("outer", "dp", half_sum(grad_out_t, grad_out_half, 0, heads_wide)),
    )
    output = (hidden_res + total_of(mlp_parts)).astype(bf16)
    (gain_groups,) = exchange(sizes, 7, ("gather", "tensor", total_of(gain_parts)))
    gain_sum = total_of(gain_groups)
    late = total_of(late_parts)
    grad_w_qkv = jnp.stack([late[:, i * heads_wide : (i + 1) * heads_wide] for i in range(3)])
    grad_w_out = total_of(grad_out_parts).T
    mlp_sums = jnp.concatenate(
        [total_of(mlp_sums_a), total_of(mlp_sums_b)], axis=1
    )
    grad_w_in = jnp.stack([mlp_sums[:, :hidden], mlp_sums[:, hidden : 2 * hidden]])
    grad_w_down = mlp_sums[:, 2 * hidden : 3 * hidden].T
    return (
        output,
        input_grad,
        gain_sum[0, :block],
        grad_w_qkv,
        grad_w_out,
        gain_sum[1, :block],
        grad_w_in,
        grad_w_down,
    )


def solution(mesh):
    in_specs = (
        P(("dp", "tensor"), None),
        P("dp"),
        P(None, "dp", "tensor"),
        P("tensor", "dp"),
        P("dp"),
        P(None, "dp", "tensor"),
        P("tensor", "dp"),
        P(("dp", "tensor"), None),
    )
    out_specs = (
        P(("dp", "tensor"), None),
        P(("dp", "tensor"), None),
        P("dp"),
        P(None, "dp", "tensor"),
        P("tensor", "dp"),
        P("dp"),
        P(None, "dp", "tensor"),
        P("tensor", "dp"),
    )
    sizes = {axis: mesh.shape[axis] for axis in ("dp", "tensor")}
    return jax.shard_map(functools.partial(body, sizes), mesh=mesh, in_specs=in_specs, out_specs=out_specs, check_vma=False)
```
